32 devices in a mesh: groups: 2 (over y), gx: 4 (over x, core), gy: 4 (over z).
Axes of the slice: x: 2, y: 2, z: 4, core: 2. Of those that a mesh axis runs over, the one named last changes fastest.
Arguments:
- data_a: float32 [256, 64, 256], P(('groups', 'gx'), 'gy'), parts along dimension 0
- data_b: float32 [256, 64, 256], P(('groups', 'gx'), 'gy'), parts along dimension 0
- estimate: float32 [256, 64, 256], P(('groups', 'gx'), 'gy'), parts along dimension 0, may hold values from 0.5 to 2
- psf_a: float32 [3, 31], replicated, may hold values from 0.02 to 1
- psf_b: float32 [3, 31], replicated, may hold values from 0.02 to 1
- partner: int32 [8, 4], P(('groups', 'gx'), 'gy'), parts along dimension 0, may hold values from 0 to 3, as said below
- row_shift: int32 [8, 4], P(('groups', 'gx'), 'gy'), parts along dimension 0, may hold values from 0 to 1
Outputs:
- refined: float32 [256, 64, 256], P(('groups', 'gx'), 'gy'), parts along dimension 0
The draws below stay inside these ranges and needn't reach their ends.
There are 2 independent parts, one for each index of `groups`. The reference program is written for one: setup_inputs(seed, part) draws one part's arguments, and reference() takes and returns one part's arrays. A program takes and returns all parts, laid end to end along the dimension named above; an argument that names none is the same for every part. Nothing has to cross between parts.
Inputs may be any that keep to these rules, and one draw needn't show every extreme that they name: partner[i, j] = i XOR m_j, where m_j, one of 1 to 3, is shared by all i of the column j; a stored tile keeps its y position. The stored tile of view B for region tile (a, b) holds the region's planes moved cyclically toward higher z by 128 * row_shift[a, b].
All inputs are finite; a program needn't handle non-finite values.
Results may differ from the reference program's by a relative error of at most 0.00002.
Values sent between devices are 32-bit elements; how exact they have to be, the bound alone decides.
A program may use at most 64 MiB of HBM per device.

```python
import math
import jax
import jax.numpy as jnp
from jax import lax

CX = 32
CY = 16
DEPTH = 256
TAPS = 31
ZB = 128
ITERS = 2
NX = 128
NY = 64
N_GX = 4
N_GY = 4


def draw_data_a(key, part):
    rough = jnp.exp(jax.random.uniform(jax.random.fold_in(key, 11), (NX, NY, DEPTH), jnp.float32, -1.5, 1.5))
    return rough


def draw_data_b(key, part):
    rough = jnp.exp(jax.random.uniform(jax.random.fold_in(key, 23), (NX, NY, DEPTH), jnp.float32, -1.5, 1.5))
    return rough


def draw_partner(key, part):
    xor_masks = jax.random.randint(jax.random.fold_in(key, 37), (N_GY,), 1, N_GX, dtype=jnp.int32)
    return jnp.bitwise_xor(jnp.arange(N_GX, dtype=jnp.int32)[:, None], xor_masks[None, :])


def set_ends(result, own_key, low, largest):
    place = [jax.random.randint(jax.random.fold_in(own_key, axis), (), 0, length) for axis, length in enumerate(result.shape)]
    widest = result.shape.index(max(result.shape))
    next_to = place[:widest] + [(place[widest] + 1) % result.shape[widest]] + place[widest + 1:]
    return result.at[tuple(place)].set(low).at[tuple(next_to)].set(largest)


def level_of(rng, shape, pieces, smallest, largest):
    def one(axis_at, parts):
        steps = jax.random.uniform(jax.random.fold_in(jax.random.fold_in(rng, 6), axis_at), (parts,), jnp.float32, smallest / len(pieces), largest / len(pieces))
        return jnp.repeat(jnp.exp(steps), shape[axis_at] // parts).reshape((-1,) + (1,) * (len(shape) - axis_at - 1))

    level = one(*pieces[0])
    for cut in pieces[1:]:
        level = level * one(*cut)
    return level


def setup_inputs(seed: int = 0, part: int = 0) -> dict:
    splits = jax.random.split(jax.random.key(seed), 8)
    own_keys = jax.random.split(jax.random.fold_in(splits[7], part), 8)
    data_a = draw_data_a(jax.random.fold_in(jax.random.fold_in(splits[7], part), 71), part)
    data_b = draw_data_b(jax.random.fold_in(jax.random.fold_in(splits[7], part), 71), part)
    estimate = jnp.clip(jnp.exp(math.log(2.0) - 1.3862944 * jax.random.uniform(own_keys[2], (NX, NY, DEPTH), jnp.float32) ** level_of(own_keys[2], (NX, NY, DEPTH), ((0, 4), (1, 4)), -0.2, 0.2)), 0.5, 2.0)
    psf_a = jnp.clip(jnp.exp(jax.random.uniform(splits[3], (3, TAPS), jnp.float32, math.log(0.02), math.log(1.0))), 0.02, 1.0)
    psf_b = jnp.clip(jnp.exp(jax.random.uniform(splits[4], (3, TAPS), jnp.float32, math.log(0.02), math.log(1.0))), 0.02, 1.0)
    partner = draw_partner(jax.random.fold_in(jax.random.fold_in(splits[7], part), 71), part)
    row_shift = set_ends(jax.random.randint(own_keys[6], (N_GX, N_GY), 0, DEPTH // ZB), jax.random.fold_in(own_keys[6], 1), 0, (DEPTH // ZB) - 1).astype(jnp.int32)
    return {"data_a": data_a, "data_b": data_b, "estimate": estimate, "psf_a": psf_a, "psf_b": psf_b, "partner": partner, "row_shift": row_shift}


def kernels(psf):
    return psf / jnp.sum(psf, axis=1, keepdims=True)


def slide(padded, taps, axis_dim, extent, mirror):
    radius = (taps.shape[0] - 1) // 2
    summed = None
    for tap_index in range(taps.shape[0]):
        begin = tap_index if mirror else 2 * radius - tap_index
        piece = taps[tap_index] * lax.slice_in_dim(padded, begin, begin + extent, axis=axis_dim)
        summed = piece if summed is None else summed + piece
    return summed


def widen(volume, axis_dim, radius):
    padding = [(0, 0), (0, 0), (0, 0)]
    padding[axis_dim] = (radius, radius)
    return jnp.pad(volume, padding)


def filtered(volume, kernel, mirror):
    radius = (kernel.shape[1] - 1) // 2
    along_z = slide(widen(volume, 2, radius), kernel[2], 2, volume.shape[2], mirror)
    along_x = slide(widen(along_z, 0, radius), kernel[0], 0, volume.shape[0], mirror)
    return slide(widen(along_x, 1, radius), kernel[1], 1, volume.shape[1], mirror)


def coverage(taps, begin, extent, whole):
    radius = (taps.shape[0] - 1) // 2
    places = begin + jnp.arange(extent, dtype=jnp.int32)
    summed = jnp.zeros((extent,), taps.dtype)
    for tap_index in range(taps.shape[0]):
        source = places - radius + tap_index
        inside = (source >= 0) & (source < whole)
        summed = summed + jnp.where(inside, taps[tap_index], 0.0)
    return summed


def edge_weight(kernel):
    first = coverage(kernel[0], 0, NX, NX)
    second = coverage(kernel[1], 0, NY, NY)
    third = coverage(kernel[2], 0, DEPTH, DEPTH)
    return (first[:, None, None] * second[None, :, None]) * third[None, None, :]


def reference(data_a, data_b, estimate, psf_a, psf_b, partner, row_shift):
    kernel_a = kernels(psf_a)
    kernel_b = kernels(psf_b)
    weight_a = edge_weight(kernel_a)
    weight_b = edge_weight(kernel_b)
    stored = data_b.reshape(N_GX, CX, N_GY, CY, DEPTH)
    columns = jnp.arange(N_GY, dtype=jnp.int32)[None, :]
    picked = stored[partner.astype(jnp.int32), :, columns, :, :]
    moved = jnp.transpose(picked, (0, 2, 1, 3, 4)).reshape(NX, NY, DEPTH)
    offsets = jnp.repeat(jnp.repeat(row_shift.astype(jnp.int32), CX, axis=0), CY, axis=1) * ZB
    planes = (jnp.arange(DEPTH, dtype=jnp.int32)[None, None, :] + offsets[:, :, None]) % DEPTH
    view_b = jnp.take_along_axis(moved, planes.astype(jnp.int32), axis=2)
    refined = estimate
    for step_index in range(ITERS):
        refined = (refined * filtered(data_a / filtered(refined, kernel_a, False), kernel_a, True)) / weight_a
        refined = (refined * filtered(view_b / filtered(refined, kernel_b, False), kernel_b, True)) / weight_b
    return refined
```

```python
import jax
import jax.numpy as jnp
from jax import lax
from jax.experimental import pallas as pl
from jax.experimental.pallas import tpu as pltpu
from jax.sharding import PartitionSpec as P

ZB = 128
ITERS = 2
CH = 4
MESH = pl.DeviceIdType.MESH
F32 = jnp.float32
BF16 = jnp.bfloat16


def split(x):
    hi = x.astype(BF16)
    lo = (x - hi.astype(F32)).astype(BF16)
    return hi, lo


GROUP = 2 * CH
KEPT = CH - 1
CARRIERS = [i for i in range(GROUP) if i != KEPT]


def tap_matrix(kern, row, index, taps):
    out = jnp.zeros(index.shape, F32)
    for k in range(taps):
        out = jnp.where(index == k, kern[row : row + 1, k : k + 1], out)
    return out


def kernel(
    n_x, n_y,
    partner_hbm, shift_hbm, psf_a_hbm, psf_b_hbm, data_a_hbm, data_b_hbm, est_hbm,
    out_ref,
    partner_ref, shift_ref, psf_a_ref, psf_b_ref, data_b_ref,
    ybuf, upbuf, downbuf, xbuf, data, moved, chosen, zhi, zlo, ymat, gtab, r0tab,
    y_send, y_recv, x_send, x_recv, m_send, m_recv, in_sem, small_sem, est_sem,
):
    X, Y, Z = est_hbm.shape
    taps = psf_a_hbm.shape[1]
    R = (taps - 1) // 2
    H = Y
    W = R + 1
    T = Y // 2
    n_ch = X // CH
    half = n_ch // 2
    par = lax.rem(lax.axis_index("gx"), 2)

    def at(a, b):
        return a + par * (X - a - b)

    def chunk(t):
        return at(t * CH, t * CH + CH)

    def ready(t):
        return (t * CH, t * CH + KEPT) if t % 2 == 0 else (t * CH - 1, t * CH + CH)

    smalls = [
        pltpu.make_async_copy(src, dst, small_sem.at[i])
        for i, (src, dst) in enumerate(
            [(psf_a_hbm, psf_a_ref), (psf_b_hbm, psf_b_ref), (partner_hbm, partner_ref), (shift_hbm, shift_ref)]
        )
    ]
    loads = []
    for t in range(n_ch):
        rows = pl.ds(chunk(t), CH)
        loads.append(
            pltpu.make_async_copy(est_hbm.at[rows], ybuf.at[0, rows, pl.ds(Y, Y), :], est_sem.at[t])
        )
    bulk = [
        pltpu.make_async_copy(data_b_hbm, data_b_ref, in_sem.at[0]),
        pltpu.make_async_copy(data_a_hbm, data.at[0], in_sem.at[1]),
    ]
    for copy in smalls + loads + bulk:
        copy.start()

    bits = n_x.bit_length() - 1
    gx = lax.axis_index("gx")
    gy = lax.axis_index("gy")
    has = {"l": gx > 0, "r": gx < n_x - 1, "d": gy > 0, "u": gy < n_y - 1}
    where = {"l": {"gx": gx - 1}, "r": {"gx": gx + 1}, "d": {"gy": gy - 1}, "u": {"gy": gy + 1}}

    def mate(b):
        bit = lax.rem(lax.div(gx, 1 << b), 2)
        return {"gx": gx + (1 - 2 * bit) * (1 << b)}

    barrier = pltpu.get_barrier_semaphore()
    count = bits
    for side in "lrdu":
        count = count + has[side].astype(jnp.int32)

        @pl.when(has[side])
        def _(side=side):
            pl.semaphore_signal(barrier, inc=1, device_id=where[side], device_id_type=MESH)

    for b in range(bits):
        pl.semaphore_signal(barrier, inc=1, device_id=mate(b), device_id_type=MESH)

    near = gx - 1 + 2 * par
    far = gx + 1 - 2 * par
    has_near = (near >= 0) & (near < n_x)

    def y_copy(slot, t, side, part):
        d = 0 if side == "d" else 1
        first, last = t * CH, t * CH + CH
        top, count = 0, Y
        if part == 1:
            first, top, count = first + KEPT, (0 if side == "d" else T), T
        elif t % 2 == 0:
            last = first + KEPT
        rows = pl.ds(at(first, last), last - first)
        return pltpu.make_async_remote_copy(
            src_ref=(downbuf if side == "d" else upbuf).at[slot, rows, pl.ds(top, count), :],
            dst_ref=ybuf.at[slot, rows, pl.ds((H + Y if side == "d" else 0) + top, count), :],
            send_sem=y_send.at[slot, t, d, part],
            recv_sem=y_recv.at[slot, t, d, part],
            device_id=where[side],
            device_id_type=MESH,
        )

    def parts(t):
        return (0, 1) if t % 2 == 0 else (0,)

    def carriers(t):
        group = t // 2 * GROUP
        kept = at(group + KEPT, group + KEPT + 1)
        return kept, [(j, at(group + i, group + i + 1)) for j, i in enumerate(CARRIERS) if i // CH == t % 2]

    def y_start(slot, t, own):
        rows = pl.ds(chunk(t), CH)
        upbuf[slot, rows] = own
        downbuf[slot, rows] = own
        kept, planes = carriers(t)
        for j, plane in planes:
            upbuf[slot, plane, 0:1, :] = ybuf[slot, kept, H + 1 + j : H + 2 + j, :]
            downbuf[slot, plane, Y - 1 : Y, :] = ybuf[slot, kept, H + T + j : H + T + 1 + j, :]
        for side in "du":

            @pl.when(has[side])
            def _(side=side):
                for part in parts(t):
                    y_copy(slot, t, side, part).start()

    def y_wait(slot, t):
        for side, other in (("d", "u"), ("u", "d")):

            @pl.when(has[other])
            def _(side=side):
                for part in parts(t):
                    y_copy(slot, t, side, part).wait_recv()

        for side in "du":

            @pl.when(has[side])
            def _(side=side):
                for part in parts(t):
                    y_copy(slot, t, side, part).wait_send()

        if t % 2 == 1:
            for kept, planes in (carriers(t - 1), carriers(t)):
                for j, plane in planes:
                    ybuf[slot, kept, 1 + j : 2 + j, :] = ybuf[slot, plane, 0:1, :]
                    low = H + Y + T + j
                    ybuf[slot, kept, low : low + 1, :] = ybuf[slot, plane, H + 2 * Y - 1 : H + 2 * Y, :]

    def x_copy(slot, t, parity):
        a, b = ready(t)
        first = W + a + parity * (X - a - b)
        right = parity if t < half else 1 - parity
        to = first + X - 2 * X * right
        return pltpu.make_async_remote_copy(
            src_ref=xbuf.at[slot, pl.ds(first, b - a)],
            dst_ref=xbuf.at[slot, pl.ds(to, b - a)],
            send_sem=x_send.at[slot, t],
            recv_sem=x_recv.at[slot, t],
            device_id={"gx": near if t < half else far},
            device_id_type=MESH,
        )

    def x_when(t, act):
        if t < half:
            pl.when(has_near)(act)
        else:
            act()

    def x_start(slot, t):
        x_when(t, lambda: x_copy(slot, t, par).start())

    def x_wait(slot, t):
        x_when(t, lambda: x_copy(slot, t, 1 - par).wait_recv())

    def x_wait_send(slot):
        for t in range(n_ch):
            x_when(t, lambda t=t: x_copy(slot, t, par).wait_send())

    def m_copy(b, q):
        rows = pl.ds(q * CH, CH)
        return pltpu.make_async_remote_copy(
            src_ref=(data_b_ref if b == 0 else chosen.at[b - 1]).at[rows],
            dst_ref=moved.at[b, rows],
            send_sem=m_send.at[b, q],
            recv_sem=m_recv.at[b, q],
            device_id=mate(b),
            device_id_type=MESH,
        )

    def tables(view, corr):
        psf = (psf_b_ref if view else psf_a_ref)[...]
        kern = psf / jnp.sum(psf, axis=1, keepdims=True)
        zin = lax.broadcasted_iota(jnp.int32, (Z, Z), 0)
        zout = lax.broadcasted_iota(jnp.int32, (Z, Z), 1)
        full = tap_matrix(kern, 2, (zin - zout + R) if corr else (zout - zin + R), taps)
        if corr:
            full = full / jnp.sum(full, axis=0, keepdims=True)
        zhi[view, corr], zlo[view, corr] = split(full)

        wide = 2 * H + Y
        col = lax.broadcasted_iota(jnp.int32, (Y, 3 * wide), 1)
        yout = lax.broadcasted_iota(jnp.int32, (Y, 3 * wide), 0)
        yin = col - jnp.where(col >= 2 * wide, 2 * wide, jnp.where(col >= wide, wide, 0)) - H
        full = tap_matrix(kern, 1, (yin - yout + R) if corr else (yout - yin + R), taps)
        if corr:
            place = gy * Y + yin
            inside = (place >= 0) & (place < n_y * Y) & (col < wide)
            full = full / jnp.sum(jnp.where(inside, full, 0.0), axis=1, keepdims=True)
        hi, lo = split(full)
        ymat[view, corr] = jnp.where(col < 2 * wide, hi.astype(F32), lo.astype(F32)).astype(BF16)

        for j in range(taps):
            k = j if corr else taps - 1 - j
            gtab[view, corr, j] = jnp.broadcast_to(kern[0:1, k : k + 1], (Y, Z))
        if corr:
            place = gx * X - R + lax.broadcasted_iota(jnp.int32, (X, 1, Z), 0)
            e0 = jnp.zeros((X, 1, Z), F32)
            for k in range(taps):
                inside = (place + k >= 0) & (place + k < n_x * X)
                e0 = e0 + jnp.where(inside, gtab[view, corr, k, 0:1, :][None], 0.0)
            r0tab[view] = jnp.broadcast_to(1.0 / e0, (X, Y, Z))

    smalls[0].wait()
    smalls[1].wait()
    tables(0, 0)

    for g in range(X // GROUP):
        kept = at(g * GROUP + KEPT, g * GROUP + KEPT + 1)
        for slot in range(2):
            ybuf[slot, kept, 0:1, :] = jnp.zeros((1, Z), F32)
            ybuf[slot, kept, H + 2 * Y - 1 : H + 2 * Y, :] = jnp.zeros((1, Z), F32)

    @pl.when(gy == 0)
    def _():
        ybuf[:, :, 0:H, :] = jnp.zeros((2, X, H, Z), F32)

    @pl.when(gy == n_y - 1)
    def _():
        ybuf[:, :, H + Y :, :] = jnp.zeros((2, X, H, Z), F32)

    @pl.when(gx == 0)
    def _():
        xbuf[:, 0:W] = jnp.zeros((2, W, Y, Z), F32)

    @pl.when(gx == n_x - 1)
    def _():
        xbuf[:, W + X :] = jnp.zeros((2, W, Y, Z), F32)

    pl.semaphore_wait(barrier, count)
    for t in range(n_ch):
        loads[t].wait()
        y_start(0, t, ybuf[0, pl.ds(chunk(t), CH), H : H + Y, :])
    bulk[0].wait()
    for q in range(n_ch):
        m_copy(0, q).start()
    tables(0, 1)
    tables(1, 0)
    tables(1, 1)
    smalls[2].wait()
    smalls[3].wait()
    bulk[1].wait()

    mask = jnp.bitwise_xor(partner_ref[0, 0], gx)

    def pick(b):
        for q in range(n_ch):
            m_copy(b, q).wait()
        old = data_b_ref[...] if b == 0 else chosen[b - 1]
        bit = jnp.bitwise_and(jnp.right_shift(mask, b), 1)
        new = jnp.where(jnp.full((1, 1, 1), bit) == 1, moved[b], old)
        if b == bits - 1:
            turned = jnp.concatenate([new[:, :, ZB:], new[:, :, :ZB]], axis=2)
            data[1] = jnp.where(jnp.full((1, 1, 1), shift_ref[0, 0]) == 1, turned, new)
        else:
            chosen[b] = new
            if b > 0:
                for q in range(n_ch):
                    m_copy(b + 1, q).start()

    def inner(view, slot, t):
        y_wait(slot, t)
        a, b = ready(t)
        size = b - a
        first = at(a, b)
        mat = ymat[view, slot]
        outs = []
        for x in range(size):
            hi, lo = split(ybuf[slot, first + x])
            outs.append(
                jnp.dot(mat, jnp.concatenate([hi, lo, hi], axis=0), preferred_element_type=F32)
            )
        hi, lo = split(jnp.concatenate(outs, axis=0))
        top = zhi[view, slot]
        res = (
            jnp.dot(hi, top, preferred_element_type=F32)
            + jnp.dot(lo, top, preferred_element_type=F32)
            + jnp.dot(hi, zlo[view, slot], preferred_element_type=F32)
        )
        xbuf[slot, pl.ds(W + first, size)] = res.reshape(size, Y, Z)
        x_start(slot, t)

    def along_x(view, slot, t):
        first = chunk(t)
        total = None
        for j in range(taps):
            term = gtab[view, slot, j][None] * xbuf[slot, pl.ds(first + 1 + j, CH)]
            total = term if total is None else total + term
        return total

    def passes(p, view, slot, finish):
        made = 0
        for t in range(n_ch):
            inner(view, slot, t)
            if bits > 1 and t >= half:

                @pl.when(p == 0)
                def _(q=slot * half + t - half):
                    m_copy(1, q).start()

            while made < half and (made + 1) * CH + R <= ready(t)[1]:
                if made == 0:
                    for n in range(half):
                        x_wait(slot, n)
                finish(made)
                made += 1
        for n in range(half, n_ch):
            x_wait(slot, n)
        for t in range(made, n_ch):
            finish(t)
        x_wait_send(slot)

    def step(p, carry):
        view = lax.rem(p, 2)

        @pl.when(p == 0)
        def _():
            pick(0)

        @pl.when(p == 1)
        def _():
            for b in range(1, bits):
                pick(b)

        def ratio(t):
            rows = pl.ds(chunk(t), CH)
            new = data[view, rows] / along_x(view, 0, t)
            ybuf[1, rows, H : H + Y, :] = new
            y_start(1, t, new)

        def update(t):
            rows = pl.ds(chunk(t), CH)
            new = ybuf[0, rows, H : H + Y, :] * along_x(view, 1, t) * r0tab[view, rows]
            ybuf[0, rows, H : H + Y, :] = new

            @pl.when(p < 2 * ITERS - 1)
            def _():
                y_start(0, t, new)

        passes(p, view, 0, ratio)
        passes(p, view, 1, update)
        return carry

    lax.fori_loop(0, 2 * ITERS, step, 0)
    out_ref[...] = ybuf[0, :, H : H + Y, :]


def solution(mesh):
    n_x, n_y = mesh.shape["gx"], mesh.shape["gy"]

    def body(data_a, data_b, estimate, psf_a, psf_b, partner, row_shift):
        X, Y, Z = estimate.shape
        taps = psf_a.shape[1]
        R = (taps - 1) // 2
        n_ch = X // CH
        bits = n_x.bit_length() - 1
        vmem = pl.BlockSpec(memory_space=pltpu.VMEM)
        hbm = pl.BlockSpec(memory_space=pltpu.HBM)
        sem = pltpu.SemaphoreType.DMA
        return pl.pallas_call(
            lambda *refs: kernel(n_x, n_y, *refs),
            out_shape=jax.ShapeDtypeStruct((X, Y, Z), F32),
            in_specs=[hbm] * 7,
            out_specs=vmem,
            scratch_shapes=[
                pltpu.SMEM((1, 1), jnp.int32),
                pltpu.SMEM((1, 1), jnp.int32),
                pltpu.VMEM((3, taps), F32),
                pltpu.VMEM((3, taps), F32),
                pltpu.VMEM((X, Y, Z), F32),
                pltpu.VMEM((2, X, 3 * Y, Z), F32),
                pltpu.VMEM((2, X, Y, Z), F32),
                pltpu.VMEM((2, X, Y, Z), F32),
                pltpu.VMEM((2, X + 2 * (R + 1), Y, Z), F32),
                pltpu.VMEM((2, X, Y, Z), F32),
                pltpu.VMEM((bits, X, Y, Z), F32),
                pltpu.VMEM((max(bits - 1, 1), X, Y, Z), F32),
                pltpu.VMEM((2, 2, Z, Z), BF16),
                pltpu.VMEM((2, 2, Z, Z), BF16),
                pltpu.VMEM((2, 2, Y, 9 * Y), BF16),
                pltpu.VMEM((2, 2, taps, Y, Z), F32),
                pltpu.VMEM((2, X, Y, Z), F32),
                sem((2, n_ch, 2, 2)),
                sem((2, n_ch, 2, 2)),
                sem((2, n_ch)),
                sem((2, n_ch)),
                sem((bits, n_ch)),
                sem((bits, n_ch)),
                sem((2,)),
                sem((4,)),
                sem((n_ch,)),
            ],
            compiler_params=pltpu.CompilerParams(
                collective_id=0, has_side_effects=True, vmem_limit_bytes=60 << 20
            ),
        )(partner, row_shift, psf_a, psf_b, data_a, data_b, estimate)

    tile = P(("groups", "gx"), "gy", None)
    small = P(("groups", "gx"), "gy")
    return jax.shard_map(
        body,
        mesh=mesh,
        in_specs=(tile, tile, tile, P(), P(), small, small),
        out_specs=tile,
        check_vma=False,
    )
```

```python
import jax
import jax.numpy as jnp
from jax import lax
from jax.experimental import pallas as pl
from jax.experimental.pallas import tpu as pltpu
from jax.sharding import PartitionSpec as P

ZB = 128
ITERS = 2
CH = 4
MESH = pl.DeviceIdType.MESH
F32 = jnp.float32
BF16 = jnp.bfloat16


def split(x):
    hi = x.astype(BF16)
    lo = (x - hi.astype(F32)).astype(BF16)
    return hi, lo


GROUP = 2 * CH
KEPT = CH - 1
CARRIERS = [i for i in range(GROUP) if i != KEPT]


def tap_matrix(kern, row, index, taps):
    out = jnp.zeros(index.shape, F32)
    for k in range(taps):
        out = jnp.where(index == k, kern[row : row + 1, k : k + 1], out)
    return out


def kernel(
    n_x, n_y,
    partner_hbm, shift_hbm, psf_a_hbm, psf_b_hbm, data_a_hbm, data_b_hbm, est_hbm,
    out_ref,
    partner_ref, shift_ref, psf_a_ref, psf_b_ref, data_b_ref,
    ybuf, upbuf, downbuf, xbuf, data, moved, chosen, zhi, zlo, ymat, gtab, r0tab,
    y_send, y_recv, x_send, x_recv, m_send, m_recv, in_sem, small_sem, est_sem,
):
    X, Y, Z = est_hbm.shape
    taps = psf_a_hbm.shape[1]
    R = (taps - 1) // 2
    H = Y
    W = R + 1
    T = Y // 2
    n_ch = X // CH
    half = n_ch // 2
    par = lax.rem(lax.axis_index("gx"), 2)

    def at(a, b):
        return a + par * (X - a - b)

    def chunk(t):
        return at(t * CH, t * CH + CH)

    def ready(t):
        return (t * CH, t * CH + KEPT) if t % 2 == 0 else (t * CH - 1, t * CH + CH)

    bits = n_x.bit_length() - 1
    gx = lax.axis_index("gx")
    gy = lax.axis_index("gy")
    has = {"l": gx > 0, "r": gx < n_x - 1, "d": gy > 0, "u": gy < n_y - 1}
    where = {"l": {"gx": gx - 1}, "r": {"gx": gx + 1}, "d": {"gy": gy - 1}, "u": {"gy": gy + 1}}

    def mate(b):
        bit = lax.rem(lax.div(gx, 1 << b), 2)
        return {"gx": gx + (1 - 2 * bit) * (1 << b)}

    barrier = pltpu.get_barrier_semaphore()
    count = bits
    for side in "lrdu":
        count = count + has[side].astype(jnp.int32)

        @pl.when(has[side])
        def _(side=side):
            pl.semaphore_signal(barrier, inc=1, device_id=where[side], device_id_type=MESH)

    for b in range(bits):
        pl.semaphore_signal(barrier, inc=1, device_id=mate(b), device_id_type=MESH)

    smalls = [
        pltpu.make_async_copy(src, dst, small_sem.at[i])
        for i, (src, dst) in enumerate(
            [(psf_a_hbm, psf_a_ref), (psf_b_hbm, psf_b_ref), (partner_hbm, partner_ref), (shift_hbm, shift_ref)]
        )
    ]
    loads = []
    for t in range(n_ch):
        rows = pl.ds(chunk(t), CH)
        loads.append(
            pltpu.make_async_copy(est_hbm.at[rows], ybuf.at[0, rows, pl.ds(Y, Y), :], est_sem.at[t])
        )
    bulk = [
        pltpu.make_async_copy(data_b_hbm, data_b_ref, in_sem.at[0]),
        pltpu.make_async_copy(data_a_hbm, data.at[0], in_sem.at[1]),
    ]
    for copy in smalls + loads + bulk:
        copy.start()

    near = gx - 1 + 2 * par
    far = gx + 1 - 2 * par
    has_near = (near >= 0) & (near < n_x)

    def y_copy(slot, t, side, part):
        d = 0 if side == "d" else 1
        first, last = t * CH, t * CH + CH
        top, count = 0, Y
        if part == 1:
            first, top, count = first + KEPT, (0 if side == "d" else T), T
        elif t % 2 == 0:
            last = first + KEPT
        rows = pl.ds(at(first, last), last - first)
        return pltpu.make_async_remote_copy(
            src_ref=(downbuf if side == "d" else upbuf).at[slot, rows, pl.ds(top, count), :],
            dst_ref=ybuf.at[slot, rows, pl.ds((H + Y if side == "d" else 0) + top, count), :],
            send_sem=y_send.at[slot, t, d, part],
            recv_sem=y_recv.at[slot, t, d, part],
            device_id=where[side],
            device_id_type=MESH,
        )

    def parts(t):
        return (0, 1) if t % 2 == 0 else (0,)

    def carriers(t):
        group = t // 2 * GROUP
        kept = at(group + KEPT, group + KEPT + 1)
        return kept, [(j, at(group + i, group + i + 1)) for j, i in enumerate(CARRIERS) if i // CH == t % 2]

    def y_start(slot, t, own):
        rows = pl.ds(chunk(t), CH)
        upbuf[slot, rows] = own
        downbuf[slot, rows] = own
        kept, planes = carriers(t)
        for j, plane in planes:
            upbuf[slot, plane, 0:1, :] = ybuf[slot, kept, H + 1 + j : H + 2 + j, :]
            downbuf[slot, plane, Y - 1 : Y, :] = ybuf[slot, kept, H + T + j : H + T + 1 + j, :]
        for side in "du":

            @pl.when(has[side])
            def _(side=side):
                for part in parts(t):
                    y_copy(slot, t, side, part).start()

    def y_wait(slot, t):
        for side, other in (("d", "u"), ("u", "d")):

            @pl.when(has[other])
            def _(side=side):
                for part in parts(t):
                    y_copy(slot, t, side, part).wait_recv()

        for side in "du":

            @pl.when(has[side])
            def _(side=side):
                for part in parts(t):
                    y_copy(slot, t, side, part).wait_send()

        if t % 2 == 1:
            for kept, planes in (carriers(t - 1), carriers(t)):
                for j, plane in planes:
                    ybuf[slot, kept, 1 + j : 2 + j, :] = ybuf[slot, plane, 0:1, :]
                    low = H + Y + T + j
                    ybuf[slot, kept, low : low + 1, :] = ybuf[slot, plane, H + 2 * Y - 1 : H + 2 * Y, :]

    def x_copy(slot, t, parity):
        a, b = ready(t)
        first = W + a + parity * (X - a - b)
        right = parity if t < half else 1 - parity
        to = first + X - 2 * X * right
        return pltpu.make_async_remote_copy(
            src_ref=xbuf.at[slot, pl.ds(first, b - a)],
            dst_ref=xbuf.at[slot, pl.ds(to, b - a)],
            send_sem=x_send.at[slot, t],
            recv_sem=x_recv.at[slot, t],
            device_id={"gx": near if t < half else far},
            device_id_type=MESH,
        )

    def x_when(t, act):
        if t < half:
            pl.when(has_near)(act)
        else:
            act()

    def x_start(slot, t):
        x_when(t, lambda: x_copy(slot, t, par).start())

    def x_wait(slot, t):
        x_when(t, lambda: x_copy(slot, t, 1 - par).wait_recv())

    def x_wait_send(slot):
        for t in range(n_ch):
            x_when(t, lambda t=t: x_copy(slot, t, par).wait_send())

    def m_copy(b, q):
        rows = pl.ds(q * CH, CH)
        return pltpu.make_async_remote_copy(
            src_ref=(data_b_ref if b == 0 else chosen.at[b - 1]).at[rows],
            dst_ref=moved.at[b, rows],
            send_sem=m_send.at[b, q],
            recv_sem=m_recv.at[b, q],
            device_id=mate(b),
            device_id_type=MESH,
        )

    def tables(view, corr):
        psf = (psf_b_ref if view else psf_a_ref)[...]
        kern = psf / jnp.sum(psf, axis=1, keepdims=True)
        zin = lax.broadcasted_iota(jnp.int32, (Z, Z), 0)
        zout = lax.broadcasted_iota(jnp.int32, (Z, Z), 1)
        full = tap_matrix(kern, 2, (zin - zout + R) if corr else (zout - zin + R), taps)
        if corr:
            full = full / jnp.sum(full, axis=0, keepdims=True)
        zhi[view, corr], zlo[view, corr] = split(full)

        wide = 2 * H + Y
        col = lax.broadcasted_iota(jnp.int32, (Y, 3 * wide), 1)
        yout = lax.broadcasted_iota(jnp.int32, (Y, 3 * wide), 0)
        yin = col - jnp.where(col >= 2 * wide, 2 * wide, jnp.where(col >= wide, wide, 0)) - H
        full = tap_matrix(kern, 1, (yin - yout + R) if corr else (yout - yin + R), taps)
        if corr:
            place = gy * Y + yin
            inside = (place >= 0) & (place < n_y * Y) & (col < wide)
            full = full / jnp.sum(jnp.where(inside, full, 0.0), axis=1, keepdims=True)
        hi, lo = split(full)
        ymat[view, corr] = jnp.where(col < 2 * wide, hi.astype(F32), lo.astype(F32)).astype(BF16)

        for j in range(taps):
            k = j if corr else taps - 1 - j
            gtab[view, corr, j] = jnp.broadcast_to(kern[0:1, k : k + 1], (Y, Z))
        if corr:
            place = gx * X - R + lax.broadcasted_iota(jnp.int32, (X, 1, Z), 0)
            e0 = jnp.zeros((X, 1, Z), F32)
            for k in range(taps):
                inside = (place + k >= 0) & (place + k < n_x * X)
                e0 = e0 + jnp.where(inside, gtab[view, corr, k, 0:1, :][None], 0.0)
            r0tab[view] = jnp.broadcast_to(1.0 / e0, (X, Y, Z))

    smalls[0].wait()
    smalls[1].wait()
    tables(0, 0)

    for g in range(X // GROUP):
        kept = at(g * GROUP + KEPT, g * GROUP + KEPT + 1)
        for slot in range(2):
            ybuf[slot, kept, 0:1, :] = jnp.zeros((1, Z), F32)
            ybuf[slot, kept, H + 2 * Y - 1 : H + 2 * Y, :] = jnp.zeros((1, Z), F32)

    @pl.when(gy == 0)
    def _():
        ybuf[:, :, 0:H, :] = jnp.zeros((2, X, H, Z), F32)

    @pl.when(gy == n_y - 1)
    def _():
        ybuf[:, :, H + Y :, :] = jnp.zeros((2, X, H, Z), F32)

    @pl.when(gx == 0)
    def _():
        xbuf[:, 0:W] = jnp.zeros((2, W, Y, Z), F32)

    @pl.when(gx == n_x - 1)
    def _():
        xbuf[:, W + X :] = jnp.zeros((2, W, Y, Z), F32)

    pl.semaphore_wait(barrier, count)
    for t in range(n_ch):
        loads[t].wait()
        y_start(0, t, ybuf[0, pl.ds(chunk(t), CH), H : H + Y, :])
    bulk[0].wait()
    for q in range(n_ch):
        m_copy(0, q).start()
    tables(0, 1)
    tables(1, 0)
    tables(1, 1)
    smalls[2].wait()
    smalls[3].wait()
    bulk[1].wait()

    mask = jnp.bitwise_xor(partner_ref[0, 0], gx)

    def pick(b):
        for q in range(n_ch):
            m_copy(b, q).wait()
        old = data_b_ref[...] if b == 0 else chosen[b - 1]
        bit = jnp.bitwise_and(jnp.right_shift(mask, b), 1)
        new = jnp.where(jnp.full((1, 1, 1), bit) == 1, moved[b], old)
        if b == bits - 1:
            turned = jnp.concatenate([new[:, :, ZB:], new[:, :, :ZB]], axis=2)
            data[1] = jnp.where(jnp.full((1, 1, 1), shift_ref[0, 0]) == 1, turned, new)
        else:
            chosen[b] = new
            if b > 0:
                for q in range(n_ch):
                    m_copy(b + 1, q).start()

    def inner(view, slot, t):
        y_wait(slot, t)
        a, b = ready(t)
        size = b - a
        first = at(a, b)
        mat = ymat[view, slot]
        outs = []
        for x in range(size):
            hi, lo = split(ybuf[slot, first + x])
            outs.append(
                jnp.dot(mat, jnp.concatenate([hi, lo, hi], axis=0), preferred_element_type=F32)
            )
        hi, lo = split(jnp.concatenate(outs, axis=0))
        top = zhi[view, slot]
        res = (
            jnp.dot(hi, top, preferred_element_type=F32)
            + jnp.dot(lo, top, preferred_element_type=F32)
            + jnp.dot(hi, zlo[view, slot], preferred_element_type=F32)
        )
        xbuf[slot, pl.ds(W + first, size)] = res.reshape(size, Y, Z)
        x_start(slot, t)

    def along_x(view, slot, t):
        first = chunk(t)
        total = None
        for j in range(taps):
            term = gtab[view, slot, j][None] * xbuf[slot, pl.ds(first + 1 + j, CH)]
            total = term if total is None else total + term
        return total

    def passes(p, view, slot, finish):
        made = 0
        for t in range(n_ch):
            inner(view, slot, t)
            if bits > 1 and t >= half:

                @pl.when(p == 0)
                def _(q=slot * half + t - half):
                    m_copy(1, q).start()

            while made < half and (made + 1) * CH + R <= ready(t)[1]:
                if made == 0:
                    for n in range(half):
                        x_wait(slot, n)
                finish(made)
                made += 1
        for n in range(half, n_ch):
            x_wait(slot, n)
        for t in range(made, n_ch):
            finish(t)
        x_wait_send(slot)

    def step(p, carry):
        view = lax.rem(p, 2)

        @pl.when(p == 0)
        def _():
            pick(0)

        @pl.when(p == 1)
        def _():
            for b in range(1, bits):
                pick(b)

        def ratio(t):
            rows = pl.ds(chunk(t), CH)
            new = data[view, rows] / along_x(view, 0, t)
            ybuf[1, rows, H : H + Y, :] = new
            y_start(1, t, new)

        def update(t):
            rows = pl.ds(chunk(t), CH)
            new = ybuf[0, rows, H : H + Y, :] * along_x(view, 1, t) * r0tab[view, rows]
            ybuf[0, rows, H : H + Y, :] = new

            @pl.when(p < 2 * ITERS - 1)
            def _():
                y_start(0, t, new)

            @pl.when(p == 2 * ITERS - 1)
            def _():
                out_ref[rows] = new

        passes(p, view, 0, ratio)
        passes(p, view, 1, update)
        return carry

    lax.fori_loop(0, 2 * ITERS, step, 0)


def solution(mesh):
    n_x, n_y = mesh.shape["gx"], mesh.shape["gy"]

    def body(data_a, data_b, estimate, psf_a, psf_b, partner, row_shift):
        X, Y, Z = estimate.shape
        taps = psf_a.shape[1]
        R = (taps - 1) // 2
        n_ch = X // CH
        bits = n_x.bit_length() - 1
        vmem = pl.BlockSpec(memory_space=pltpu.VMEM)
        hbm = pl.BlockSpec(memory_space=pltpu.HBM)
        sem = pltpu.SemaphoreType.DMA
        return pl.pallas_call(
            lambda *refs: kernel(n_x, n_y, *refs),
            out_shape=pltpu.VMEM((X, Y, Z), F32),
            in_specs=[hbm] * 7,
            out_specs=vmem,
            scratch_shapes=[
                pltpu.SMEM((1, 1), jnp.int32),
                pltpu.SMEM((1, 1), jnp.int32),
                pltpu.VMEM((3, taps), F32),
                pltpu.VMEM((3, taps), F32),
                pltpu.VMEM((X, Y, Z), F32),
                pltpu.VMEM((2, X, 3 * Y, Z), F32),
                pltpu.VMEM((2, X, Y, Z), F32),
                pltpu.VMEM((2, X, Y, Z), F32),
                pltpu.VMEM((2, X + 2 * (R + 1), Y, Z), F32),
                pltpu.VMEM((2, X, Y, Z), F32),
                pltpu.VMEM((bits, X, Y, Z), F32),
                pltpu.VMEM((max(bits - 1, 1), X, Y, Z), F32),
                pltpu.VMEM((2, 2, Z, Z), BF16),
                pltpu.VMEM((2, 2, Z, Z), BF16),
                pltpu.VMEM((2, 2, Y, 9 * Y), BF16),
                pltpu.VMEM((2, 2, taps, Y, Z), F32),
                pltpu.VMEM((2, X, Y, Z), F32),
                sem((2, n_ch, 2, 2)),
                sem((2, n_ch, 2, 2)),
                sem((2, n_ch)),
                sem((2, n_ch)),
                sem((bits, n_ch)),
                sem((bits, n_ch)),
                sem((2,)),
                sem((4,)),
                sem((n_ch,)),
            ],
            compiler_params=pltpu.CompilerParams(
                collective_id=0, has_side_effects=True, vmem_limit_bytes=60 << 20
            ),
        )(partner, row_shift, psf_a, psf_b, data_a, data_b, estimate)

    tile = P(("groups", "gx"), "gy", None)
    small = P(("groups", "gx"), "gy")
    return jax.shard_map(
        body,
        mesh=mesh,
        in_specs=(tile, tile, tile, P(), P(), small, small),
        out_specs=tile,
        check_vma=False,
    )
```

```python
import jax
import jax.numpy as jnp
from jax import lax
from jax.experimental import pallas as pl
from jax.experimental.pallas import tpu as pltpu
from jax.sharding import PartitionSpec as P

ZB = 128
ITERS = 2
CH = 4
MESH = pl.DeviceIdType.MESH
F32 = jnp.float32
BF16 = jnp.bfloat16


def split(x):
    hi = x.astype(BF16)
    lo = (x - hi.astype(F32)).astype(BF16)
    return hi, lo


GROUP = 2 * CH
KEPT = CH - 1
CARRIERS = [i for i in range(GROUP) if i != KEPT]


def tap_matrix(kern, row, index, taps):
    out = jnp.zeros(index.shape, F32)
    for k in range(taps):
        out = jnp.where(index == k, kern[row : row + 1, k : k + 1], out)
    return out


def kernel(
    n_x, n_y,
    partner_hbm, shift_hbm, psf_a_hbm, psf_b_hbm, data_a_hbm, data_b_hbm, est_hbm,
    out_ref,
    partner_ref, shift_ref, psf_a_ref, psf_b_ref, data_b_ref,
    ybuf, upbuf, downbuf, xbuf, data, moved, chosen, zhi, zlo, ymat, gtab, r0tab,
    y_send, y_recv, x_send, x_recv, m_send, m_recv, in_sem, small_sem, est_sem,
):
    X, Y, Z = est_hbm.shape
    taps = psf_a_hbm.shape[1]
    R = (taps - 1) // 2
    H = Y
    W = R + 1
    T = Y // 2
    n_ch = X // CH
    half = n_ch // 2
    par = lax.rem(lax.axis_index("gx"), 2)

    def at(a, b):
        return a + par * (X - a - b)

    def chunk(t):
        return at(t * CH, t * CH + CH)

    def ready(t):
        return (t * CH, t * CH + KEPT) if t % 2 == 0 else (t * CH - 1, t * CH + CH)

    bits = n_x.bit_length() - 1
    gx = lax.axis_index("gx")
    gy = lax.axis_index("gy")
    has = {"l": gx > 0, "r": gx < n_x - 1, "d": gy > 0, "u": gy < n_y - 1}
    where = {"l": {"gx": gx - 1}, "r": {"gx": gx + 1}, "d": {"gy": gy - 1}, "u": {"gy": gy + 1}}

    def mate(b):
        bit = lax.rem(lax.div(gx, 1 << b), 2)
        return {"gx": gx + (1 - 2 * bit) * (1 << b)}

    barrier = pltpu.get_barrier_semaphore()
    count = bits
    for side in "lrdu":
        count = count + has[side].astype(jnp.int32)

        @pl.when(has[side])
        def _(side=side):
            pl.semaphore_signal(barrier, inc=1, device_id=where[side], device_id_type=MESH)

    for b in range(bits):
        pl.semaphore_signal(barrier, inc=1, device_id=mate(b), device_id_type=MESH)

    smalls = [
        pltpu.make_async_copy(src, dst, small_sem.at[i])
        for i, (src, dst) in enumerate(
            [(psf_a_hbm, psf_a_ref), (psf_b_hbm, psf_b_ref), (partner_hbm, partner_ref), (shift_hbm, shift_ref)]
        )
    ]
    loads = []
    for t in range(n_ch):
        rows = pl.ds(chunk(t), CH)
        loads.append(
            pltpu.make_async_copy(est_hbm.at[rows], ybuf.at[0, rows, pl.ds(Y, Y), :], est_sem.at[t])
        )
    bulk = [
        pltpu.make_async_copy(data_b_hbm, data_b_ref, in_sem.at[0]),
        pltpu.make_async_copy(data_a_hbm, data.at[0], in_sem.at[1]),
    ]
    for copy in loads + smalls + bulk:
        copy.start()

    near = gx - 1 + 2 * par
    far = gx + 1 - 2 * par
    has_near = (near >= 0) & (near < n_x)

    def y_copy(slot, t, side, part):
        d = 0 if side == "d" else 1
        first, last = t * CH, t * CH + CH
        top, count = 0, Y
        if part == 1:
            first, top, count = first + KEPT, (0 if side == "d" else T), T
        elif t % 2 == 0:
            last = first + KEPT
        rows = pl.ds(at(first, last), last - first)
        return pltpu.make_async_remote_copy(
            src_ref=(downbuf if side == "d" else upbuf).at[slot, rows, pl.ds(top, count), :],
            dst_ref=ybuf.at[slot, rows, pl.ds((H + Y if side == "d" else 0) + top, count), :],
            send_sem=y_send.at[slot, t, d, part],
            recv_sem=y_recv.at[slot, t, d, part],
            device_id=where[side],
            device_id_type=MESH,
        )

    def parts(t):
        return (0, 1) if t % 2 == 0 else (0,)

    def carriers(t):
        group = t // 2 * GROUP
        kept = at(group + KEPT, group + KEPT + 1)
        return kept, [(j, at(group + i, group + i + 1)) for j, i in enumerate(CARRIERS) if i // CH == t % 2]

    def y_stage(slot, t, own):
        rows = pl.ds(chunk(t), CH)
        upbuf[slot, rows] = own
        downbuf[slot, rows] = own
        kept, planes = carriers(t)
        for j, plane in planes:
            upbuf[slot, plane, 0:1, :] = ybuf[slot, kept, H + 1 + j : H + 2 + j, :]
            downbuf[slot, plane, Y - 1 : Y, :] = ybuf[slot, kept, H + T + j : H + T + 1 + j, :]

    def y_send_all(slot, t):
        for side in "du":

            @pl.when(has[side])
            def _(side=side):
                for part in parts(t):
                    y_copy(slot, t, side, part).start()

    def y_start(slot, t, own):
        y_stage(slot, t, own)
        y_send_all(slot, t)

    def y_wait(slot, t):
        for side, other in (("d", "u"), ("u", "d")):

            @pl.when(has[other])
            def _(side=side):
                for part in parts(t):
                    y_copy(slot, t, side, part).wait_recv()

        for side in "du":

            @pl.when(has[side])
            def _(side=side):
                for part in parts(t):
                    y_copy(slot, t, side, part).wait_send()

        if t % 2 == 1:
            for kept, planes in (carriers(t - 1), carriers(t)):
                for j, plane in planes:
                    ybuf[slot, kept, 1 + j : 2 + j, :] = ybuf[slot, plane, 0:1, :]
                    low = H + Y + T + j
                    ybuf[slot, kept, low : low + 1, :] = ybuf[slot, plane, H + 2 * Y - 1 : H + 2 * Y, :]

    def x_copy(slot, t, parity):
        a, b = ready(t)
        first = W + a + parity * (X - a - b)
        right = parity if t < half else 1 - parity
        to = first + X - 2 * X * right
        return pltpu.make_async_remote_copy(
            src_ref=xbuf.at[slot, pl.ds(first, b - a)],
            dst_ref=xbuf.at[slot, pl.ds(to, b - a)],
            send_sem=x_send.at[slot, t],
            recv_sem=x_recv.at[slot, t],
            device_id={"gx": near if t < half else far},
            device_id_type=MESH,
        )

    def x_when(t, act):
        if t < half:
            pl.when(has_near)(act)
        else:
            act()

    def x_start(slot, t):
        x_when(t, lambda: x_copy(slot, t, par).start())

    def x_wait(slot, t):
        x_when(t, lambda: x_copy(slot, t, 1 - par).wait_recv())

    def x_wait_send(slot):
        for t in range(n_ch):
            x_when(t, lambda t=t: x_copy(slot, t, par).wait_send())

    def m_copy(b, q):
        rows = pl.ds(q * CH, CH)
        return pltpu.make_async_remote_copy(
            src_ref=(data_b_ref if b == 0 else chosen.at[b - 1]).at[rows],
            dst_ref=moved.at[b, rows],
            send_sem=m_send.at[b, q],
            recv_sem=m_recv.at[b, q],
            device_id=mate(b),
            device_id_type=MESH,
        )

    def tables(view, corr):
        psf = (psf_b_ref if view else psf_a_ref)[...]
        kern = psf / jnp.sum(psf, axis=1, keepdims=True)
        zin = lax.broadcasted_iota(jnp.int32, (Z, Z), 0)
        zout = lax.broadcasted_iota(jnp.int32, (Z, Z), 1)
        full = tap_matrix(kern, 2, (zin - zout + R) if corr else (zout - zin + R), taps)
        if corr:
            full = full / jnp.sum(full, axis=0, keepdims=True)
        zhi[view, corr], zlo[view, corr] = split(full)

        wide = 2 * H + Y
        col = lax.broadcasted_iota(jnp.int32, (Y, 3 * wide), 1)
        yout = lax.broadcasted_iota(jnp.int32, (Y, 3 * wide), 0)
        yin = col - jnp.where(col >= 2 * wide, 2 * wide, jnp.where(col >= wide, wide, 0)) - H
        full = tap_matrix(kern, 1, (yin - yout + R) if corr else (yout - yin + R), taps)
        if corr:
            place = gy * Y + yin
            inside = (place >= 0) & (place < n_y * Y) & (col < wide)
            full = full / jnp.sum(jnp.where(inside, full, 0.0), axis=1, keepdims=True)
        hi, lo = split(full)
        ymat[view, corr] = jnp.where(col < 2 * wide, hi.astype(F32), lo.astype(F32)).astype(BF16)

        for j in range(taps):
            k = j if corr else taps - 1 - j
            gtab[view, corr, j] = jnp.broadcast_to(kern[0:1, k : k + 1], (Y, Z))
        if corr:
            place = gx * X - R + lax.broadcasted_iota(jnp.int32, (X, 1, Z), 0)
            e0 = jnp.zeros((X, 1, Z), F32)
            for k in range(taps):
                inside = (place + k >= 0) & (place + k < n_x * X)
                e0 = e0 + jnp.where(inside, gtab[view, corr, k, 0:1, :][None], 0.0)
            r0tab[view] = jnp.broadcast_to(1.0 / e0, (X, Y, Z))

    for g in range(X // GROUP):
        kept = at(g * GROUP + KEPT, g * GROUP + KEPT + 1)
        for slot in range(2):
            ybuf[slot, kept, 0:1, :] = jnp.zeros((1, Z), F32)
            ybuf[slot, kept, H + 2 * Y - 1 : H + 2 * Y, :] = jnp.zeros((1, Z), F32)

    @pl.when(gy == 0)
    def _():
        ybuf[:, :, 0:H, :] = jnp.zeros((2, X, H, Z), F32)

    @pl.when(gy == n_y - 1)
    def _():
        ybuf[:, :, H + Y :, :] = jnp.zeros((2, X, H, Z), F32)

    @pl.when(gx == 0)
    def _():
        xbuf[:, 0:W] = jnp.zeros((2, W, Y, Z), F32)

    @pl.when(gx == n_x - 1)
    def _():
        xbuf[:, W + X :] = jnp.zeros((2, W, Y, Z), F32)

    for t in range(n_ch):
        loads[t].wait()
        y_stage(0, t, ybuf[0, pl.ds(chunk(t), CH), H : H + Y, :])
    pl.semaphore_wait(barrier, count)
    for t in range(n_ch):
        y_send_all(0, t)
    bulk[0].wait()
    for q in range(n_ch):
        m_copy(0, q).start()
    smalls[0].wait()
    smalls[1].wait()
    tables(0, 0)
    tables(0, 1)
    tables(1, 0)
    tables(1, 1)
    smalls[2].wait()
    smalls[3].wait()
    bulk[1].wait()

    mask = jnp.bitwise_xor(partner_ref[0, 0], gx)

    def pick(b):
        for q in range(n_ch):
            m_copy(b, q).wait()
        old = data_b_ref[...] if b == 0 else chosen[b - 1]
        bit = jnp.bitwise_and(jnp.right_shift(mask, b), 1)
        new = jnp.where(jnp.full((1, 1, 1), bit) == 1, moved[b], old)
        if b == bits - 1:
            turned = jnp.concatenate([new[:, :, ZB:], new[:, :, :ZB]], axis=2)
            data[1] = jnp.where(jnp.full((1, 1, 1), shift_ref[0, 0]) == 1, turned, new)
        else:
            chosen[b] = new
            if b > 0:
                for q in range(n_ch):
                    m_copy(b + 1, q).start()

    def inner(view, slot, t):
        y_wait(slot, t)
        a, b = ready(t)
        size = b - a
        first = at(a, b)
        mat = ymat[view, slot]
        outs = []
        for x in range(size):
            hi, lo = split(ybuf[slot, first + x])
            outs.append(
                jnp.dot(mat, jnp.concatenate([hi, lo, hi], axis=0), preferred_element_type=F32)
            )
        hi, lo = split(jnp.concatenate(outs, axis=0))
        top = zhi[view, slot]
        res = (
            jnp.dot(hi, top, preferred_element_type=F32)
            + jnp.dot(lo, top, preferred_element_type=F32)
            + jnp.dot(hi, zlo[view, slot], preferred_element_type=F32)
        )
        xbuf[slot, pl.ds(W + first, size)] = res.reshape(size, Y, Z)
        x_start(slot, t)

    def along_x(view, slot, t):
        first = chunk(t)
        total = None
        for j in range(taps):
            term = gtab[view, slot, j][None] * xbuf[slot, pl.ds(first + 1 + j, CH)]
            total = term if total is None else total + term
        return total

    def passes(p, view, slot, finish):
        made = 0
        for t in range(n_ch):
            inner(view, slot, t)
            if bits > 1 and t >= half:

                @pl.when(p == 0)
                def _(q=slot * half + t - half):
                    m_copy(1, q).start()

            while made < half and (made + 1) * CH + R <= ready(t)[1]:
                if made == 0:
                    for n in range(half):
                        x_wait(slot, n)
                finish(made)
                made += 1
        for n in range(half, n_ch):
            x_wait(slot, n)
        for t in range(made, n_ch):
            finish(t)
        x_wait_send(slot)

    def step(p, carry):
        view = lax.rem(p, 2)

        @pl.when(p == 0)
        def _():
            pick(0)

        @pl.when(p == 1)
        def _():
            for b in range(1, bits):
                pick(b)

        def ratio(t):
            rows = pl.ds(chunk(t), CH)
            new = data[view, rows] / along_x(view, 0, t)
            ybuf[1, rows, H : H + Y, :] = new
            y_start(1, t, new)

        def update(t):
            rows = pl.ds(chunk(t), CH)
            new = ybuf[0, rows, H : H + Y, :] * along_x(view, 1, t) * r0tab[view, rows]
            ybuf[0, rows, H : H + Y, :] = new

            @pl.when(p < 2 * ITERS - 1)
            def _():
                y_start(0, t, new)

            @pl.when(p == 2 * ITERS - 1)
            def _():
                out_ref[rows] = new

        passes(p, view, 0, ratio)
        passes(p, view, 1, update)
        return carry

    lax.fori_loop(0, 2 * ITERS, step, 0)


def solution(mesh):
    n_x, n_y = mesh.shape["gx"], mesh.shape["gy"]

    def body(data_a, data_b, estimate, psf_a, psf_b, partner, row_shift):
        X, Y, Z = estimate.shape
        taps = psf_a.shape[1]
        R = (taps - 1) // 2
        n_ch = X // CH
        bits = n_x.bit_length() - 1
        vmem = pl.BlockSpec(memory_space=pltpu.VMEM)
        hbm = pl.BlockSpec(memory_space=pltpu.HBM)
        sem = pltpu.SemaphoreType.DMA
        return pl.pallas_call(
            lambda *refs: kernel(n_x, n_y, *refs),
            out_shape=pltpu.VMEM((X, Y, Z), F32),
            in_specs=[hbm] * 7,
            out_specs=vmem,
            scratch_shapes=[
                pltpu.SMEM((1, 1), jnp.int32),
                pltpu.SMEM((1, 1), jnp.int32),
                pltpu.VMEM((3, taps), F32),
                pltpu.VMEM((3, taps), F32),
                pltpu.VMEM((X, Y, Z), F32),
                pltpu.VMEM((2, X, 3 * Y, Z), F32),
                pltpu.VMEM((2, X, Y, Z), F32),
                pltpu.VMEM((2, X, Y, Z), F32),
                pltpu.VMEM((2, X + 2 * (R + 1), Y, Z), F32),
                pltpu.VMEM((2, X, Y, Z), F32),
                pltpu.VMEM((bits, X, Y, Z), F32),
                pltpu.VMEM((max(bits - 1, 1), X, Y, Z), F32),
                pltpu.VMEM((2, 2, Z, Z), BF16),
                pltpu.VMEM((2, 2, Z, Z), BF16),
                pltpu.VMEM((2, 2, Y, 9 * Y), BF16),
                pltpu.VMEM((2, 2, taps, Y, Z), F32),
                pltpu.VMEM((2, X, Y, Z), F32),
                sem((2, n_ch, 2, 2)),
                sem((2, n_ch, 2, 2)),
                sem((2, n_ch)),
                sem((2, n_ch)),
                sem((bits, n_ch)),
                sem((bits, n_ch)),
                sem((2,)),
                sem((4,)),
                sem((n_ch,)),
            ],
            compiler_params=pltpu.CompilerParams(
                collective_id=0, has_side_effects=True, vmem_limit_bytes=60 << 20
            ),
        )(partner, row_shift, psf_a, psf_b, data_a, data_b, estimate)

    tile = P(("groups", "gx"), "gy", None)
    small = P(("groups", "gx"), "gy")
    return jax.shard_map(
        body,
        mesh=mesh,
        in_specs=(tile, tile, tile, P(), P(), small, small),
        out_specs=tile,
        check_vma=False,
    )
```
